32 devices in a mesh: section: 4 (over z), token: 4 (over x, core), feature: 2 (over y).
Axes of the slice: x: 2, y: 2, z: 4, core: 2. Of those that a mesh axis runs over, the one named last changes fastest.
Arguments:
- residual: bfloat16 [4, 2048, 4608], P('section', 'token'), may hold values from -6 to 6
- encoder: bfloat16 [4, 4608, 8192], P('section', None, 'feature'), may hold values from -0.09375 to 0.09375
- encoder_bias: float32 [4, 8192], P('section', 'feature'), may hold values from -0.6 to 0.3
- decoder: bfloat16 [4, 4, 8192, 4608], P('section', 'token', None, 'feature'), may hold values from -0.125 to 0.125
- active: int32 [4, 32, 16], P('section'), may hold values from 0 to 3
Outputs:
- activations: bfloat16 [4, 2048, 8192], P('section', 'token', 'feature')
- reconstruction: bfloat16 [4, 2048, 4608], P('token', 'section', 'feature')
The draws below stay inside these ranges and needn't reach their ends.
Inputs may be any that keep to these rules, and one draw needn't show every extreme that they name: Which of the 4 blocks of a group is active, for each section and tile of 64 tokens.
All inputs are finite; a program needn't handle non-finite values.
Results may differ from the reference program's by a relative error of at most 0.0049.
Values may be sent and summed in bfloat16 or wider, within the bound.
A program may use at most 256 MiB of HBM per device.

```python
import jax
import jax.numpy as jnp

D = 4608
F = 8192
G = 16
BPG = 4
TILE = 64
BLOCK = 128
SECTIONS = 4
TOKENS = 2048
TILES = 32


def plant(result, key, low, top_value):
    extent = result.shape
    spot = [jax.random.randint(jax.random.fold_in(key, axis), (), 0, extent[axis]) for axis in range(len(extent))]
    result = result.at[tuple(spot)].set(low)
    longest = extent.index(max(extent))
    spot[longest] = (spot[longest] + 1) % extent[longest]
    return result.at[tuple(spot)].set(top_value)


def level_of(stream_key, dims, shards, least, largest):
    loudness = 1.0
    for axis_at, shards_of in shards:
        heights = jax.random.uniform(jax.random.fold_in(jax.random.fold_in(stream_key, 6), axis_at), (shards_of,), jnp.float32, least / len(shards), largest / len(shards))
        loudness = loudness * jnp.repeat(jnp.exp(heights), dims[axis_at] // shards_of).reshape((-1,) + (1,) * (len(dims) - 1 - axis_at))
    return loudness


def centred(own_key, extent, width, limit, split=(), held_as=jnp.bfloat16):
    array = width * jax.random.normal(own_key, extent, jnp.float32)
    if split:
        array = array * level_of(own_key, extent, split, -0.22, 0.18)
    return jnp.clip(array, -limit, limit).astype(held_as)


def setup_inputs(seed: int = 0) -> dict:
    streams_of = jax.random.split(jax.random.key(seed), 6)
    return {
        "residual": centred(streams_of[0], (SECTIONS, TOKENS, D), 1.0, 6.0, ((0, 4), (1, 4))),
        "encoder": centred(streams_of[1], (SECTIONS, D, F), D ** -0.5, 0.09375, ((0, 4), (2, 2))),
        "encoder_bias": jnp.clip(-0.6 + 0.90000004 * jax.random.uniform(streams_of[2], (SECTIONS, F), jnp.float32) ** level_of(streams_of[2], (SECTIONS, F), ((0, 4), (1, 2)), -0.2, 0.2), -0.6, 0.3),
        "decoder": centred(streams_of[3], (SECTIONS, SECTIONS, F, D), (G * BLOCK) ** -0.5, 0.125, ((0, 4), (1, 4), (3, 2))),
        "active": plant(jax.random.randint(streams_of[4], (SECTIONS, TILES, G), 0, BPG), jax.random.fold_in(streams_of[4], 1), 0, BPG - 1).astype(jnp.int32),
    }


def reference(residual, encoder, encoder_bias, decoder, active):
    token_total = residual.shape[1]
    feature_ids = jnp.arange(F, dtype=jnp.int32)
    group_of = feature_ids // (BPG * BLOCK)
    within = (feature_ids // BLOCK) % BPG
    tile_of = jnp.arange(token_total, dtype=jnp.int32) // TILE
    all_codes = []
    all_sparse = []
    for source in range(SECTIONS):
        hidden = jnp.dot(residual[source], encoder[source], preferred_element_type=jnp.float32) + encoder_bias[source]
        feature_codes = jax.nn.relu(hidden).astype(jnp.bfloat16)
        chosen = active[source][tile_of][:, group_of]
        keep_mask = chosen == within[None, :]
        sparse = jnp.where(keep_mask, feature_codes, jnp.zeros_like(feature_codes))
        all_codes.append(feature_codes)
        all_sparse.append(sparse)
    all_rebuilt = []
    for target in range(SECTIONS):
        running = jnp.zeros((token_total, residual.shape[2]), jnp.float32)
        for source in range(target + 1):
            running = running + jnp.dot(all_sparse[source], decoder[source, target], preferred_element_type=jnp.float32)
        all_rebuilt.append(running.astype(jnp.bfloat16))
    return jnp.stack(all_codes), jnp.stack(all_rebuilt)
```

```python
import functools

import jax
import jax.numpy as jnp
from jax import lax
from jax.experimental import pallas as pl
from jax.experimental.pallas import tpu as pltpu
from jax.sharding import PartitionSpec as P

G = 16
BPG = 4
TILE = 64
BLOCK = 128
PIECES = 4


def column_block(width, most):
    best = width
    for size in range(BLOCK, most + 1, BLOCK):
        if width % size == 0:
            best = size
    return best


def encode_kernel(active_ref, residual_ref, encoder_ref, bias_ref, codes_ref, compact_ref):
    group = pl.program_id(0)
    rows = residual_ref.shape[0]
    half = 2 * BLOCK
    for at in range(0, BPG * BLOCK, half):
        hidden = jnp.dot(
            residual_ref[...], encoder_ref[:, at : at + half], preferred_element_type=jnp.float32
        )
        hidden = hidden + bias_ref[:, at : at + half]
        codes_ref[:, at : at + half] = jnp.maximum(hidden, 0.0).astype(codes_ref.dtype)
    for tile in range(rows // TILE):
        span = slice(tile * TILE, (tile + 1) * TILE)
        chosen = active_ref[tile, group]
        start = pl.multiple_of(chosen * BLOCK, BLOCK)
        compact_ref[span, :] = codes_ref[span, pl.ds(start, BLOCK)]


def encode(residual, encoder, encoder_bias, own_active):
    rows, depth = residual.shape[1:]
    width = encoder.shape[2]
    groups = width // (BPG * BLOCK)
    wide = BPG * BLOCK
    return pl.pallas_call(
        encode_kernel,
        grid=(groups,),
        in_specs=[
            pl.BlockSpec(memory_space=pltpu.SMEM),
            pl.BlockSpec((None, rows, depth), lambda g: (0, 0, 0)),
            pl.BlockSpec((None, depth, wide), lambda g: (0, 0, g)),
            pl.BlockSpec((1, wide), lambda g: (0, g)),
        ],
        out_specs=[
            pl.BlockSpec((None, rows, wide), lambda g: (0, 0, g)),
            pl.BlockSpec((rows, BLOCK), lambda g: (0, g)),
        ],
        out_shape=[
            jax.ShapeDtypeStruct((1, rows, width), jnp.bfloat16),
            jax.ShapeDtypeStruct((rows, groups * BLOCK), jnp.bfloat16),
        ],
        compiler_params=pltpu.CompilerParams(vmem_limit_bytes=40 * 2**20),
        cost_estimate=pl.CostEstimate(
            flops=2 * rows * depth * width,
            bytes_accessed=2 * (rows * depth + depth * width + rows * width),
            transcendentals=0,
        ),
        name="encode",
    )(own_active, residual, encoder, encoder_bias)


def decode_kernel(places, rows, tiles_per_place, first_tile, meta_ref, active_ref, codes_ref, weight_ref, *rest):
    out_refs, dense = rest[:places], rest[places]
    shards = codes_ref.shape[0] // places
    groups_local = codes_ref.shape[2] // BLOCK
    in_range = meta_ref[places] == 1

    @pl.when(jnp.logical_and(pl.program_id(0) == 0, in_range))
    def _():
        def fill(step, carry):
            slot = step // (rows // TILE)
            tile = step % (rows // TILE)
            place = meta_ref[slot]
            source = pl.ds(pl.multiple_of(tile * TILE, TILE), TILE)
            target = pl.ds(pl.multiple_of(step * TILE, TILE), TILE)
            for shard in range(shards):
                for local in range(groups_local):
                    group = shard * groups_local + local
                    value = codes_ref[place * shards + shard, source, local * BLOCK : (local + 1) * BLOCK]
                    chosen = active_ref[place * tiles_per_place + first_tile + tile, group]
                    for block in range(BPG):
                        at = (group * BPG + block) * BLOCK
                        dense[target, at : at + BLOCK] = jnp.where(
                            chosen == block, value, jnp.zeros_like(value)
                        )
            return carry

        lax.fori_loop(0, places * (rows // TILE), fill, 0)

    @pl.when(in_range)
    def _():
        decoded = jnp.dot(dense[...], weight_ref[...], preferred_element_type=jnp.float32)
        for slot in range(places):
            out_refs[slot][...] = decoded[slot * rows : (slot + 1) * rows].astype(jnp.bfloat16)

    @pl.when(jnp.logical_not(in_range))
    def _():
        for slot in range(places):
            out_refs[slot][...] = jnp.zeros_like(out_refs[slot])


def decode(meta, active, codes, decoder, places, rows, tiles_per_place, first_tile):
    depth, width = decoder.shape[2:]
    block = column_block(width, 2 * BLOCK)
    return pl.pallas_call(
        functools.partial(decode_kernel, places, rows, tiles_per_place, first_tile),
        grid=(width // block,),
        in_specs=[
            pl.BlockSpec(memory_space=pltpu.SMEM),
            pl.BlockSpec(memory_space=pltpu.SMEM),
            pl.BlockSpec(codes.shape, lambda n: (0, 0, 0)),
            pl.BlockSpec((None, None, depth, block), lambda n: (0, 0, 0, n)),
        ],
        out_specs=[pl.BlockSpec((rows, block), lambda n: (0, n))] * places,
        out_shape=[jax.ShapeDtypeStruct((rows, width), jnp.bfloat16)] * places,
        scratch_shapes=[pltpu.VMEM((places * rows, depth), jnp.bfloat16)],
        compiler_params=pltpu.CompilerParams(vmem_limit_bytes=40 * 2**20),
        cost_estimate=pl.CostEstimate(
            flops=2 * places * rows * depth * width,
            bytes_accessed=2 * (codes.size + depth * width + places * rows * width),
            transcendentals=0,
        ),
        name="decode",
    )(meta, active, codes, decoder)


def orders(count):
    return [
        sorted(range(count), key=lambda d: (-abs(d - z), -d)) for z in range(count)
    ]


def pick(section, values, indices):
    chosen = values[indices[0]]
    for z in range(1, len(indices)):
        if indices[z] != indices[z - 1]:
            chosen = jnp.where(section >= z, values[indices[z]], chosen)
    return chosen


def fill_gaps(indices):
    known = [i for i in indices if i is not None]
    last = known[0]
    filled = []
    for i in indices:
        last = last if i is None else i
        filled.append(last)
    return filled


def add(value, arrived):
    if arrived is None:
        return value
    return (value.astype(jnp.float32) + arrived.astype(jnp.float32)).astype(jnp.bfloat16)


class Line:
    def __init__(self, section, count, values):
        self.section, self.count, self.values = section, count, values
        self.step = 0
        self.up = self.down = None

    def operands(self):
        table = orders(self.count)
        far = self.count - 1 - self.step
        ups = [table[z].index(z + far) if z + far < self.count else None for z in range(self.count)]
        downs = [table[z].index(z - far) if z - far >= 0 else None for z in range(self.count)]
        return (
            add(pick(self.section, self.values, fill_gaps(ups)), self.up),
            add(pick(self.section, self.values, fill_gaps(downs)), self.down),
        )

    def send(self, up, down):
        far = self.count - 1 - self.step
        self.up = lax.ppermute(up, "section", [(z, z + 1) for z in range(self.count - far)])
        self.down = lax.ppermute(down, "section", [(z, z - 1) for z in range(far, self.count)])
        self.step += 1

    def total(self):
        total = self.values[-1].astype(jnp.float32)
        total = total + self.up.astype(jnp.float32) + self.down.astype(jnp.float32)
        return total.astype(jnp.bfloat16)


def body(residual, encoder, encoder_bias, decoder, active):
    section = lax.axis_index("section")
    token_place = lax.axis_index("token")
    feature_place = lax.axis_index("feature")
    sections = lax.axis_size("section")
    feature_count = lax.axis_size("feature")
    rows_here = residual.shape[1]
    groups_local = G // feature_count
    tile_count = rows_here // TILE
    assert lax.axis_size("token") == sections
    own_active = lax.dynamic_slice(
        active[0],
        (token_place * tile_count, feature_place * groups_local),
        (tile_count, groups_local),
    )
    codes, compact = encode(residual, encoder, encoder_bias, own_active)
    order = jnp.asarray(orders(sections), jnp.int32)
    order = lax.dynamic_slice(order, (section, 0), (1, sections))[0]
    in_range = (token_place >= section).astype(jnp.int32)
    meta = jnp.concatenate([order, in_range[None]])
    rows = rows_here // PIECES
    gathered = [
        lax.all_gather(
            compact[piece * rows : (piece + 1) * rows], ("token", "feature"), axis=0, tiled=False
        )
        for piece in range(PIECES)
    ]
    lines = []
    for slot in range(PIECES + sections - 2):
        if slot < PIECES:
            values = decode(
                meta, active[0], gathered[slot], decoder, sections, rows, tile_count, slot * rows // TILE
            )
            lines.append(Line(section, sections, values))
        moving = [line for line in lines if line.step < sections - 1]
        pairs = [line.operands() for line in moving]
        if slot + 1 < PIECES:
            gathered[slot + 1], pairs = lax.optimization_barrier((gathered[slot + 1], pairs))
        for line, (up, down) in zip(moving, pairs):
            line.send(up, down)
    rebuilt = [line.total() for line in lines]
    return (codes, jnp.concatenate(rebuilt, axis=0)[None])


def solution(mesh):
    placed = (
        P("section", "token", None),
        P("section", None, "feature"),
        P("section", "feature"),
        P("section", "token", None, "feature"),
        P("section", None, None),
    )
    return jax.shard_map(
        body,
        mesh=mesh,
        in_specs=placed,
        out_specs=(P("section", "token", "feature"), P("token", "section", "feature")),
        check_vma=False,
    )
```
